32 devices in a mesh: dp: 16 (over z, y, x), tile: 2 (over core).
Axes of the slice: x: 2, y: 2, z: 4, core: 2. Of those that a mesh axis runs over, the one named last changes fastest.
Arguments:
- layer_input: bfloat16 [49152, 768], P(('dp', 'tile')), may hold values from -32 to 32
- segment_ids: int32 [49152], P(('dp', 'tile')), may hold values from 0 to 11, as said below
- pad_mask: int32 [49152], P(('dp', 'tile')), may hold values from 0 to 1, as said below
- pair_slots: int32 [192, 2], P('dp'), may hold values from 0 to 23, as said below
- result_cotangent: bfloat16 [49152, 768], P(('dp', 'tile')), may hold values from -0.059814453 to 0.059814453
- query_weight: bfloat16 [768, 768], P(('dp', 'tile')), may hold values from -0.21875 to 0.21875
- key_weight: bfloat16 [768, 768], P(('dp', 'tile')), may hold values from -0.21875 to 0.21875
- value_weight: bfloat16 [768, 768], P(('dp', 'tile')), may hold values from -0.21875 to 0.21875
- output_weight: bfloat16 [768, 768], P(('dp', 'tile')), may hold values from -0.875 to 0.875
- query_bias: bfloat16 [768], P(('dp', 'tile')), may hold values from -3 to 3
- value_bias: bfloat16 [768], P(('dp', 'tile')), may hold values from -0.59765625 to 0.59765625
- output_bias: bfloat16 [768], P(('dp', 'tile')), may hold values from -1.796875 to 1.796875
- first_gain: bfloat16 [768], P(('dp', 'tile')), may hold values from 0.5 to 1.5
- first_shift: bfloat16 [768], P(('dp', 'tile')), may hold values from -0.59765625 to 0.59765625
- inner_weight: bfloat16 [768, 3072], P(('dp', 'tile')), may hold values from -0.21875 to 0.21875
- inner_bias: bfloat16 [3072], P(('dp', 'tile')), may hold values from -1.796875 to 1.796875
- outer_weight: bfloat16 [3072, 768], P(('dp', 'tile')), may hold values from -0.109375 to 0.109375
- outer_bias: bfloat16 [768], P(('dp', 'tile')), may hold values from -1.1953125 to 1.1953125
- second_gain: bfloat16 [768], P(('dp', 'tile')), may hold values from 0.5 to 1.5
- second_shift: bfloat16 [768], P(('dp', 'tile')), may hold values from -0.59765625 to 0.59765625
Outputs:
- total_loss: float32 [], replicated
- dim_losses: float32 [5], replicated
- layer_out: bfloat16 [49152, 768], P(('dp', 'tile'))
- input_grad: float32 [49152, 768], P(('dp', 'tile'))
- query_weight_grad: float32 [768, 768], P(('dp', 'tile'))
- key_weight_grad: float32 [768, 768], P(('dp', 'tile'))
- value_weight_grad: float32 [768, 768], P(('dp', 'tile'))
- output_weight_grad: float32 [768, 768], P(('dp', 'tile'))
- query_bias_grad: float32 [768], P(('dp', 'tile'))
- value_bias_grad: float32 [768], P(('dp', 'tile'))
- output_bias_grad: float32 [768], P(('dp', 'tile'))
- first_gain_grad: float32 [768], P(('dp', 'tile'))
- first_shift_grad: float32 [768], P(('dp', 'tile'))
- inner_weight_grad: float32 [768, 3072], P(('dp', 'tile'))
- inner_bias_grad: float32 [3072], P(('dp', 'tile'))
- outer_weight_grad: float32 [3072, 768], P(('dp', 'tile'))
- outer_bias_grad: float32 [768], P(('dp', 'tile'))
- second_gain_grad: float32 [768], P(('dp', 'tile'))
- second_shift_grad: float32 [768], P(('dp', 'tile'))
The draws below stay inside these ranges and needn't reach their ends.
Inputs may be any that keep to these rules, and one draw needn't show every extreme that they name: `segment_ids`: in each device's block of 1536 rows the ids never fall; every id 0 to 11 names a sentence of 8 to 512 rows with pad_mask 1; rows with pad_mask 0 come after the last sentence and carry id 12 - 1; some sentence has exactly 512 rows. `pad_mask`: 1 on a leading run of each device's block of 1536 rows, 0 after it. `pair_slots`: each aligned block of 12 rows holds every number 0 to 23 exactly once.
All inputs are finite; a program needn't handle non-finite values.
Results may differ from the reference program's by a relative error of at most 0.017.
Values may be sent and summed in bfloat16 or wider, within the bound.
No kernel may reach another device: no remote copies, remote signals or barrier semaphores. Data moves between devices by JAX's collectives and lax.ppermute only.
A program may use at most 192 MiB of HBM per device.

```python
import jax
import jax.numpy as jnp
from jax import lax

D = 768
HEADS = 12
HEAD_DIM = 64
FF = 3072
ROWS_DEV = 1536
MINLEN = 8
MAXLEN = 512
SLOTS = 12
PAIRS = 192
TOKENS = 49152


def packed_rows(key):
    base = jax.random.fold_in(key, 11)
    devices = TOKENS // ROWS_DEV
    span = (MAXLEN // MINLEN).bit_length() - 1
    first, second = jax.random.split(base)
    powers = jax.random.randint(first, (devices, SLOTS), 0, span + 1)
    raw = MINLEN * jnp.left_shift(jnp.ones((devices, SLOTS), jnp.int32), powers.astype(jnp.int32))
    half = raw // 2
    extra = jax.random.randint(second, (devices, SLOTS), 0, half + 1)
    wanted = jnp.maximum(raw - half + extra, MINLEN)
    wanted = jnp.minimum(wanted, MAXLEN)
    wanted = wanted.at[0, 0].set(MAXLEN)
    used = jnp.zeros((devices,), jnp.int32)
    ends = []
    for slot_index in range(SLOTS):
        limit = ROWS_DEV - used - MINLEN * (SLOTS - 1 - slot_index)
        length = jnp.minimum(wanted[:, slot_index], limit)
        used = used + length
        ends.append(used)
    ends = jnp.stack(ends, axis=1)
    places = jnp.arange(ROWS_DEV, dtype=jnp.int32)
    segment = jnp.sum((ends[:, :, None] <= places[None, None, :]).astype(jnp.int32), axis=1)
    segment = jnp.minimum(segment, SLOTS - 1)
    valid = (places[None, :] < used[:, None]).astype(jnp.int32)
    return (segment.reshape(-1).astype(jnp.int32), valid.reshape(-1).astype(jnp.int32))


def draw_segment_ids(key, part):
    return packed_rows(key)[0]


def draw_pad_mask(key, part):
    return packed_rows(key)[1]


def draw_pair_slots(key, part):
    groups = PAIRS // SLOTS
    group_keys = jax.random.split(jax.random.fold_in(key, 5), groups)
    orders = jax.vmap(lambda single: jax.random.permutation(single, 2 * SLOTS))(group_keys)
    return orders.reshape(PAIRS, 2).astype(jnp.int32)


def draw_layer_input(key, part):
    devices = TOKENS // ROWS_DEV
    groups = devices // 2
    segment, valid = packed_rows(key)
    orders = draw_pair_slots(key, part).reshape(groups, 2 * SLOTS)
    places = jnp.argsort(orders, axis=1).astype(jnp.int32)
    pair_of = places // 2
    device = jnp.arange(TOKENS, dtype=jnp.int32) // ROWS_DEV
    group = device // 2
    number = device % 2 * SLOTS + segment
    pair = pair_of[group, number]
    base = jax.random.fold_in(key, 23)
    first, second, third = jax.random.split(base, 3)
    topics = jnp.clip(jax.random.normal(first, (groups * SLOTS, D), jnp.float32), -4.0, 4.0)
    topic_rows = topics[group * SLOTS + pair] * valid.astype(jnp.float32)[:, None]
    noise = jnp.clip(jax.random.normal(second, (TOKENS, D), jnp.float32), -4.0, 4.0)
    width = D // devices
    order = jax.random.permutation(third, devices).astype(jnp.int32)
    column_block = jnp.arange(D, dtype=jnp.int32) // width
    factor = jnp.where(column_block[None, :] == order[device][:, None], 4.0, 1.0)
    return ((noise + topic_rows) * factor).astype(jnp.bfloat16)


def block_levels(rng, shape, cuts, low, top_value):
    level, own = 1.0, jax.random.fold_in(rng, 6)
    for dim, blocks in cuts:
        steps = jnp.exp(jax.random.uniform(jax.random.fold_in(own, dim), (blocks,), jnp.float32, low / len(cuts), top_value / len(cuts)))
        level = level * jnp.repeat(steps, shape[dim] // blocks).reshape([-1 if axis == dim else 1 for axis in range(len(shape))])
    return level


def scatter_about(rng, shape, scale, most, shards=(), kind=jnp.bfloat16):
    loudness = block_levels(rng, shape, shards, -0.22, 0.18) if shards else 1.0
    values = jax.random.normal(rng, shape, jnp.float32) * scale * loudness
    return jnp.minimum(jnp.maximum(values, -most), most).astype(kind)


def setup_inputs(seed: int = 0) -> dict:
    streams_of = jax.random.split(jax.random.key(seed), 21)
    return {
        "layer_input": draw_layer_input(jax.random.fold_in(streams_of[20], 71), 0),
        "segment_ids": draw_segment_ids(jax.random.fold_in(streams_of[20], 71), 0),
        "pad_mask": draw_pad_mask(jax.random.fold_in(streams_of[20], 71), 0),
        "pair_slots": draw_pair_slots(jax.random.fold_in(streams_of[20], 71), 0),
        "result_cotangent": scatter_about(streams_of[4], (TOKENS, D), 0.01, 0.059814453, ((0, 32),)),
        "query_weight": scatter_about(streams_of[5], (D, D), D ** -0.5, 0.21875, ((0, 32),)),
        "key_weight": scatter_about(streams_of[6], (D, D), D ** -0.5, 0.21875, ((0, 32),)),
        "value_weight": scatter_about(streams_of[7], (D, D), D ** -0.5, 0.21875, ((0, 32),)),
        "output_weight": scatter_about(streams_of[8], (D, D), (D // 16) ** -0.5, 0.875, ((0, 32),)),
        "query_bias": scatter_about(streams_of[9], (D,), 0.5, 3.0, ((0, 32),)),
        "value_bias": scatter_about(streams_of[10], (D,), 0.1, 0.59765625, ((0, 32),)),
        "output_bias": scatter_about(streams_of[11], (D,), 0.3, 1.796875, ((0, 32),)),
        "first_gain": jnp.clip(1.0 + 0.1 * jax.random.normal(streams_of[12], (D,), jnp.float32), 0.5, 1.5).astype(jnp.bfloat16),
        "first_shift": scatter_about(streams_of[13], (D,), 0.1, 0.59765625, ((0, 32),)),
        "inner_weight": scatter_about(streams_of[14], (D, FF), D ** -0.5, 0.21875, ((0, 32),)),
        "inner_bias": scatter_about(streams_of[15], (FF,), 0.3, 1.796875, ((0, 32),)),
        "outer_weight": scatter_about(streams_of[16], (FF, D), FF ** -0.5, 0.109375, ((0, 32),)),
        "outer_bias": scatter_about(streams_of[17], (D,), 0.2, 1.1953125, ((0, 32),)),
        "second_gain": jnp.clip(1.0 + 0.1 * jax.random.normal(streams_of[18], (D,), jnp.float32), 0.5, 1.5).astype(jnp.bfloat16),
        "second_shift": scatter_about(streams_of[19], (D,), 0.1, 0.59765625, ((0, 32),)),
    }


@jax.custom_vjp
def low(v):
    return lax.optimization_barrier(v.astype(jnp.bfloat16)).astype(jnp.float32)

@jax.custom_vjp
def low_back(v):
    return v

def low_keep(v):
    return (low(v), None)

def low_pass(kept, grad):
    return (grad,)

def back_keep(v):
    return (v, None)

def back_low(kept, grad):
    return (low(grad),)
low.defvjp(low_keep, low_pass)
low_back.defvjp(back_keep, back_low)
EPS_NORM = 1e-12
EPS_UNIT = 1e-06
INV_TEMP = 20.0
NEG_FILL = -1e+30
HIGH = lax.Precision.HIGHEST

def both(value):
    return low_back(low(value))

def exact_gelu(value):
    return jax.nn.gelu(value, approximate=False)

def layer_norm(value, gain, shift):
    center = value - lax.optimization_barrier(jnp.mean(value, axis=-1, keepdims=True))
    spread = lax.optimization_barrier(jnp.mean(center * center, axis=-1, keepdims=True))
    return center * lax.rsqrt(spread + EPS_NORM) * gain + shift

def unit_rows(value, width):
    front = value[:, :width]
    return front * lax.rsqrt(lax.optimization_barrier(jnp.sum(front * front, axis=1, keepdims=True)) + EPS_UNIT)

def block_forward(params, rows, segment, valid):
    query_weight, key_weight, value_weight, output_weight, query_bias, value_bias, output_bias, first_gain, first_shift, inner_weight, inner_bias, outer_weight, outer_bias, second_gain, second_shift = params
    count = rows.shape[0]
    scale = HEAD_DIM ** (-0.5)
    queries = both(jnp.dot(rows, query_weight, precision=HIGH) + query_bias).reshape(count, HEADS, HEAD_DIM)
    key_rows = both(jnp.dot(rows, key_weight, precision=HIGH)).reshape(count, HEADS, HEAD_DIM)
    value_rows = both(jnp.dot(rows, value_weight, precision=HIGH) + value_bias).reshape(count, HEADS, HEAD_DIM)
    scores = low_back(jnp.einsum('qhd,khd->hqk', queries, key_rows, precision=HIGH) * scale)
    allowed = (segment[:, None] == segment[None, :]) & (valid[None, :] == 1)
    scores = jnp.where(allowed[None], scores, NEG_FILL)
    probs = jax.nn.softmax(scores, axis=-1)
    mixed = both(jnp.einsum('hqk,khd->qhd', low(probs), value_rows, precision=HIGH)).reshape(count, D)
    branch = low_back(jnp.dot(mixed, output_weight, precision=HIGH) + output_bias)
    hidden = layer_norm(rows + branch, first_gain, first_shift)
    inner = low_back(jnp.dot(low(hidden), inner_weight, precision=HIGH) + inner_bias)
    active = low(exact_gelu(inner))
    outer = low_back(jnp.dot(active, outer_weight, precision=HIGH) + outer_bias)
    result = layer_norm(hidden + outer, second_gain, second_shift)
    member = ((segment[None, :] == jnp.arange(SLOTS, dtype=jnp.int32)[:, None]) & (valid[None, :] == 1)).astype(jnp.float32)
    counts = lax.optimization_barrier(jnp.sum(member, axis=1, keepdims=True))
    pooled = jnp.dot(member, result, precision=HIGH) / counts
    return (result, pooled)

def contrast(embeddings, pair_slots):
    group = jnp.arange(PAIRS, dtype=jnp.int32) // SLOTS * (2 * SLOTS)
    anchors = embeddings[group + pair_slots[:, 0]]
    positives = embeddings[group + pair_slots[:, 1]]
    losses = []
    for cut in (D, D * 2 // 3, D // 3, D // 6, D // 12):
        anchor_unit = unit_rows(anchors, cut)
        positive_unit = unit_rows(positives, cut)
        sims = jnp.dot(anchor_unit, positive_unit.T, precision=HIGH) * INV_TEMP
        diag = lax.optimization_barrier(jnp.sum(anchor_unit * positive_unit, axis=1)) * INV_TEMP
        row_peak = lax.optimization_barrier(jnp.max(sims, axis=1))
        row_log = row_peak + jnp.log(lax.optimization_barrier(jnp.sum(jnp.exp(sims - row_peak[:, None]), axis=1)))
        column_peak = lax.optimization_barrier(jnp.max(sims, axis=0))
        column_log = column_peak + jnp.log(lax.optimization_barrier(jnp.sum(jnp.exp(sims - column_peak[None, :]), axis=0)))
        losses.append(0.5 * (jnp.mean(row_log - diag) + jnp.mean(column_log - diag)))
    return jnp.stack(losses)

def forward(rows_all, params, segment_ids, pad_mask, pair_slots):
    blocks = rows_all.reshape(-1, ROWS_DEV, D)
    segments = segment_ids.reshape(-1, ROWS_DEV)
    valids = pad_mask.reshape(-1, ROWS_DEV)
    block_step = jax.checkpoint(block_forward)

    def step(carry, item):
        rows, segment, valid = item
        result, pooled = block_step(params, rows, segment, valid)
        return (carry, (result, pooled))
    carry, (results, pooled) = lax.scan(step, jnp.zeros((), jnp.float32), (blocks, segments, valids))
    return (results.reshape(-1, D), contrast(pooled.reshape(-1, D), pair_slots))

def reference(layer_input, segment_ids, pad_mask, pair_slots, result_cotangent, query_weight, key_weight, value_weight, output_weight, query_bias, value_bias, output_bias, first_gain, first_shift, inner_weight, inner_bias, outer_weight, outer_bias, second_gain, second_shift):
    params = tuple((weight.astype(jnp.float32) for weight in (query_weight, key_weight, value_weight, output_weight, query_bias, value_bias, output_bias, first_gain, first_shift, inner_weight, inner_bias, outer_weight, outer_bias, second_gain, second_shift)))
    rows_all = layer_input.astype(jnp.float32)

    def wrapped(rows, *weights):
        return forward(rows, weights, segment_ids, pad_mask, pair_slots)
    (result, losses), pullback = jax.vjp(wrapped, rows_all, *params)
    grads = pullback((result_cotangent.astype(jnp.float32), jnp.full((5,), PAIRS, jnp.float32)))
    return (jnp.sum(losses), losses, result.astype(jnp.bfloat16), grads[0], grads[1], grads[2], grads[3], grads[4], grads[5], grads[6], grads[7], grads[8], grads[9], grads[10], grads[11], grads[12], grads[13], grads[14], grads[15])
```

```python
import functools

import jax
import jax.numpy as jnp
from jax import lax
from jax.experimental import pallas as pl
from jax.experimental.pallas import tpu as pltpu
from jax.sharding import PartitionSpec as P

D = 768
HEADS = 12
HEAD_DIM = 64
EPS_NORM = 1e-12
EPS_UNIT = 1e-06
INV_TEMP = 20.0
NEG_FILL = -1e30
HIGH = lax.Precision.HIGHEST
F32 = jnp.float32
BF = jnp.bfloat16
NT = (((1,), (1,)), ((), ()))
TN = (((0,), (0,)), ((), ()))
FWD_TILES = (512, 512, 2)
BWD_TILES = (512, 512, 2)
PAD_SLOTS = 16


def dot(a, b):
    return jnp.dot(a, b, preferred_element_type=F32)


def nt(a, b):
    return lax.dot_general(a, b, NT, preferred_element_type=F32)


def tn(a, b):
    return lax.dot_general(a, b, TN, preferred_element_type=F32)


def digits_of(count):
    digits, stride = [], 1
    while count > 1:
        radix = 4 if count % 4 == 0 else (2 if count % 2 == 0 else count)
        digits.append((stride, radix))
        stride, count = stride * radix, count // radix
    return digits


def peer(index, stride, radix, step):
    digit = index // stride % radix
    other = digit ^ step if radix in (2, 4) else (digit + step) % radix
    return index + (other - digit) * stride


def back(index, stride, radix, step):
    digit = index // stride % radix
    other = digit ^ step if radix in (2, 4) else (digit - step) % radix
    return index + (other - digit) * stride


def send_to(value, count, stride, radix, step):
    return lax.ppermute(value, "dp", [(i, peer(i, stride, radix, step)) for i in range(count)])


def swap_tile(value):
    return lax.ppermute(value, "tile", [(0, 1), (1, 0)])


def gather_pieces(shard):
    count, me = lax.axis_size("dp"), lax.axis_index("dp")
    stack, sources = shard[None], [me]
    digits = digits_of(count)[::-1]
    for level, (stride, radix) in enumerate(digits):
        stacks, origins = [stack], [sources]
        for step in range(1, radix):
            stacks.append(send_to(stack, count, stride, radix, step))
            origins.append([back(source, stride, radix, step) for source in sources])
        if level == len(digits) - 1:
            return stacks, origins
        stack, sources = jnp.concatenate(stacks, axis=0), sum(origins, [])
    return [stack], [sources]


def place_kernel(slots, *refs, sizes):
    count = len(sizes)
    pieces, out, sems = refs[:count], refs[count], refs[count + 1]
    copies, number = [], 0
    for piece, size in zip(pieces, sizes):
        for entry in range(size):
            copies.append(pltpu.make_async_copy(piece.at[entry], out.at[slots[number]], sems.at[number]))
            number += 1
    for copy in copies:
        copy.start()
    for copy in copies:
        copy.wait()


def gather_rows(shard):
    stacks, origins = gather_pieces(shard)
    tile = lax.axis_index("tile")
    others = [swap_tile(stack) for stack in stacks]
    slots = [origin * 2 + tile for group in origins for origin in group]
    slots += [origin * 2 + (1 - tile) for group in origins for origin in group]
    sizes = [stack.shape[0] for stack in stacks] * 2
    total = sum(sizes)
    placed = pl.pallas_call(
        functools.partial(place_kernel, sizes=sizes),
        out_shape=jax.ShapeDtypeStruct((total,) + shard.shape, shard.dtype),
        grid_spec=pltpu.PrefetchScalarGridSpec(
            num_scalar_prefetch=1,
            grid=(1,),
            in_specs=[pl.BlockSpec(memory_space=pl.ANY)] * len(sizes),
            out_specs=pl.BlockSpec((total,) + shard.shape, lambda i, *_: (0, 0, 0)),
            scratch_shapes=[pltpu.SemaphoreType.DMA((total,))],
        ),
        name="place_rows",
    )(jnp.stack(slots).astype(jnp.int32), *stacks, *others)
    return placed.reshape(total * shard.shape[0], shard.shape[1])


def take(value, index, axis):
    return lax.dynamic_index_in_dim(value, index, axis, keepdims=False)


def scatter_rows(partial):
    count, me = lax.axis_size("dp"), lax.axis_index("dp")
    tile = lax.axis_index("tile")
    rows = partial.shape[0] // (2 * count)
    blocks = partial.reshape(count, 2, rows, partial.shape[1])
    got = swap_tile(take(blocks, 1 - tile, 1))
    total = take(blocks, tile, 1).astype(F32) + got.astype(F32)
    for stride, radix in digits_of(count):
        total = total.astype(BF).reshape(-1, radix, rows, partial.shape[1])
        digit = me // stride % radix
        sent = []
        for step in range(1, radix):
            other = peer(me, stride, radix, step) // stride % radix
            sent.append(send_to(take(total, other, 1), count, stride, radix, step))
        total = take(total, digit, 1).astype(F32)
        for value in sent:
            total = total + value.astype(F32)
    return total.reshape(rows, partial.shape[1])


def key_ranges(segment_ids, valid, tq, tk):
    rows = segment_ids.shape[0]
    tiles = segment_ids.reshape(rows // tq, tq)
    first, last = tiles[:, 0], tiles[:, -1]
    lo = jnp.sum((segment_ids[None, :] < first[:, None]).astype(jnp.int32), axis=1)
    hi = jnp.sum(((segment_ids[None, :] <= last[:, None]) & valid[None, :]).astype(jnp.int32), axis=1)
    return lo // tk, (hi + tk - 1) // tk


def mask_codes(segment_ids, valid, slots):
    half = 64
    ids = jnp.arange(half, dtype=jnp.int32)
    code = jnp.where(valid, segment_ids, slots)
    keys = (code[:, None] == ids[None, :]).astype(BF)
    block = (segment_ids[None, :] != ids[:, None]) & (ids[:, None] <= slots)
    queries = jnp.where(block, NEG_FILL, 0.0).astype(BF)
    return keys, queries


def fwd_kernel(lo_ref, hi_ref, q_ref, k_ref, v_ref, kc_ref, qc_ref, o_ref, lse_ref, kaug, vt, *, tq, tk):
    rows = q_ref.shape[0]
    nh = q_ref.shape[1] // 64
    kc = kc_ref[...]
    k = k_ref[...]
    for h in range(nh):
        kaug[h] = jnp.concatenate([k[:, 64 * h:64 * h + 64], kc], axis=1)
    vt[...] = v_ref[...].T

    def q_step(i, _):
        q0 = pl.multiple_of(i * tq, tq)
        qt = (q_ref[pl.ds(q0, tq), :] * jnp.asarray(0.125, BF)).T
        qc = qc_ref[:, pl.ds(q0, tq)]
        qa = [jnp.concatenate([qt[64 * h:64 * h + 64], qc], axis=0) for h in range(nh)]

        def k_step(j, carry):
            k0 = pl.multiple_of(j * tk, tk)
            out = []
            for h in range(nh):
                m, l, acc = carry[h]
                s = dot(kaug[h, pl.ds(k0, tk), :], qa[h])
                mn = jnp.maximum(m, jnp.max(s, axis=0, keepdims=True))
                alpha = jnp.exp(m - mn)
                p = jnp.exp(s - mn)
                l = l * alpha + jnp.sum(p, axis=0, keepdims=True)
                acc = acc * alpha + dot(vt[64 * h:64 * h + 64, pl.ds(k0, tk)], p.astype(BF))
                out.append((mn, l, acc))
            return tuple(out)

        init = tuple((jnp.full((1, tq), NEG_FILL, F32), jnp.zeros((1, tq), F32), jnp.zeros((64, tq), F32)) for _ in range(nh))
        res = lax.fori_loop(lo_ref[i], hi_ref[i], k_step, init)
        outs = []
        for h in range(nh):
            m, l, acc = res[h]
            outs.append(acc / l)
            lse_ref[0, h:h + 1, pl.ds(q0, tq)] = m + jnp.log(l)
        o_ref[pl.ds(q0, tq), :] = jnp.concatenate(outs, axis=0).T.astype(BF)
        return 0

    lax.fori_loop(0, rows // tq, q_step, 0)


def attend_forward(qkv, lo, hi, keys, queries, heads, tq, tk, hp):
    rows = qkv.shape[0]
    pairs = heads // 2
    steps = pairs // hp
    col = lambda off: pl.BlockSpec((rows, 128 * hp), lambda h, *_: (0, off + h))
    return pl.pallas_call(
        functools.partial(fwd_kernel, tq=tq, tk=tk),
        out_shape=(jax.ShapeDtypeStruct((rows, heads * 64), BF), jax.ShapeDtypeStruct((steps, 2 * hp, rows), F32)),
        grid_spec=pltpu.PrefetchScalarGridSpec(
            num_scalar_prefetch=2,
            grid=(steps,),
            in_specs=[col(0), col(steps), col(2 * steps),
                      pl.BlockSpec((rows, 64), lambda h, *_: (0, 0)),
                      pl.BlockSpec((64, rows), lambda h, *_: (0, 0))],
            out_specs=[pl.BlockSpec((rows, 128 * hp), lambda h, *_: (0, h)),
                       pl.BlockSpec((1, 2 * hp, rows), lambda h, *_: (h, 0, 0))],
            scratch_shapes=[pltpu.VMEM((2 * hp, rows, 128), BF), pltpu.VMEM((128 * hp, rows), BF)],
        ),
        name="attend_forward",
    )(lo, hi, qkv, qkv, qkv, keys, queries)


def bwd_kernel(lo_ref, hi_ref, q_ref, k_ref, v_ref, g_ref, o_ref, lse_ref, kc_ref, qc_ref,
               dq_ref, dk_ref, dv_ref, kaug, kt, dk, dv, *, tq, tk):
    rows = q_ref.shape[0]
    nh = q_ref.shape[1] // 64
    kc = kc_ref[...]
    k = k_ref[...]
    for h in range(nh):
        kaug[h] = jnp.concatenate([k[:, 64 * h:64 * h + 64], kc], axis=1)
    kt[...] = k.T
    dk[...] = jnp.zeros_like(dk)
    dv[...] = jnp.zeros_like(dv)
    lane = lax.broadcasted_iota(jnp.int32, (tq, 128), 1)
    sub = lax.broadcasted_iota(jnp.int32, (128, tq), 0)

    def q_step(i, _):
        q0 = pl.multiple_of(i * tq, tq)
        q = q_ref[pl.ds(q0, tq), :] * jnp.asarray(0.125, BF)
        g = g_ref[pl.ds(q0, tq), :]
        qt = q.T
        gt = g.T
        prod = gt.astype(F32) * o_ref[pl.ds(q0, tq), :].T.astype(F32)
        qc = qc_ref[:, pl.ds(q0, tq)]
        zero = jnp.zeros((), BF)
        qa, ga, delta, lse = [], [], [], []
        for h in range(nh):
            qa.append(jnp.concatenate([qt[64 * h:64 * h + 64], qc], axis=0))
            gp = gt[128 * (h // 2):128 * (h // 2) + 128]
            ga.append(jnp.where(sub // 64 == h % 2, gp, zero))
            delta.append(jnp.sum(prod[64 * h:64 * h + 64], axis=0, keepdims=True))
            lse.append(lse_ref[0, h:h + 1, pl.ds(q0, tq)])
        qz = [jnp.concatenate([jnp.where(lane // 64 == h, q[:, 128 * w:128 * w + 128], zero) for h in range(2)], axis=0) for w in range(nh // 2)]
        gz = [jnp.concatenate([jnp.where(lane // 64 == h, g[:, 128 * w:128 * w + 128], zero) for h in range(2)], axis=0) for w in range(nh // 2)]

        def k_step(j, carry):
            k0 = pl.multiple_of(j * tk, tk)
            v = v_ref[pl.ds(k0, tk), :]
            ps, dss, dqs = [], [], []
            for h in range(nh):
                s = dot(kaug[h, pl.ds(k0, tk), :], qa[h])
                dp = dot(v[:, 128 * (h // 2):128 * (h // 2) + 128], ga[h])
                p = jnp.exp(s - lse[h])
                ds = (p * (dp - delta[h])).astype(BF)
                ps.append(p.astype(BF))
                dss.append(ds)
                dqs.append(carry[h] + dot(kt[64 * h:64 * h + 64, pl.ds(k0, tk)], ds))
            for w in range(nh // 2):
                dv[pl.ds(k0, tk), 128 * w:128 * w + 128] += dot(jnp.concatenate(ps[2 * w:2 * w + 2], axis=1), gz[w])
                dk[pl.ds(k0, tk), 128 * w:128 * w + 128] += dot(jnp.concatenate(dss[2 * w:2 * w + 2], axis=1), qz[w])
            return tuple(dqs)

        res = lax.fori_loop(lo_ref[i], hi_ref[i], k_step, tuple(jnp.zeros((64, tq), F32) for _ in range(nh)))
        dq_ref[pl.ds(q0, tq), :] = (jnp.concatenate(res, axis=0) * 0.125).T.astype(BF)
        return 0

    lax.fori_loop(0, rows // tq, q_step, 0)
    dk_ref[...] = dk[...].astype(BF)
    dv_ref[...] = dv[...].astype(BF)


def attend_backward(qkv, grad, mixed, lse, lo, hi, keys, queries, heads, tq, tk, hp):
    rows = qkv.shape[0]
    pairs = heads // 2
    steps = pairs // hp
    col = lambda off: pl.BlockSpec((rows, 128 * hp), lambda h, *_: (0, off + h))
    sd = jax.ShapeDtypeStruct((rows, heads * 64), BF)
    return pl.pallas_call(
        functools.partial(bwd_kernel, tq=tq, tk=tk),
        out_shape=(sd, sd, sd),
        grid_spec=pltpu.PrefetchScalarGridSpec(
            num_scalar_prefetch=2,
            grid=(steps,),
            in_specs=[col(0), col(steps), col(2 * steps), col(0), col(0),
                      pl.BlockSpec((1, 2 * hp, rows), lambda h, *_: (h, 0, 0)),
                      pl.BlockSpec((rows, 64), lambda h, *_: (0, 0)),
                      pl.BlockSpec((64, rows), lambda h, *_: (0, 0))],
            out_specs=[pl.BlockSpec((rows, 128 * hp), lambda h, *_: (0, h))] * 3,
            scratch_shapes=[pltpu.VMEM((2 * hp, rows, 128), BF), pltpu.VMEM((128 * hp, rows), BF),
                            pltpu.VMEM((rows, 128 * hp), F32), pltpu.VMEM((rows, 128 * hp), F32)],
        ),
        name="attend_backward",
    )(lo, hi, qkv, qkv, qkv, grad, mixed, lse, keys, queries)


def exact(a, b, dims):
    return lax.dot_general(a, b, dims, precision=HIGH, preferred_element_type=F32)


def contrast_kernel(
    place_ref, own_ref, other_ref, count_ref, loss_ref, grad_ref,
    anchors, positives, product, expos, square_a, row_sum, picks, parts, sums, *, slots, widths, block,
):
    me, tile = place_ref[0], place_ref[1]
    total = own_ref.shape[0]
    blocks = total // block
    full = (((1,), (0,)), ((), ()))
    col = lax.broadcasted_iota(jnp.int32, (block, total), 1)
    base = lax.broadcasted_iota(jnp.int32, (block, total), 0)
    shift = slots * tile.astype(F32)
    away = slots * (1 - tile).astype(F32)

    def masks(index):
        row = base + index * block
        real = (row % PAD_SLOTS < slots) & (col % PAD_SLOTS < slots)
        return row, real, jnp.where((row == col) & real, 1.0, 0.0)

    def start(index):
        return pl.multiple_of(index * block, block)

    def choose(index, across):
        at = pl.ds(start(index), block)
        row, real, eye = masks(index)
        numbers = own_ref[at, D:].astype(F32)
        local = (col % PAD_SLOTS).astype(F32)
        ok = (row // PAD_SLOTS == col // PAD_SLOTS) & real
        result = []
        for which, chosen in enumerate((anchors, positives)):
            number = numbers[:, which:which + 1]
            near_own = jnp.where(ok & (number == local + shift), 1.0, 0.0).astype(BF)
            near_other = jnp.where(ok & (number == local + away), 1.0, 0.0).astype(BF)
            chosen[at, :] = (dot(near_own, own_ref[:, :D]) + dot(near_other, other_ref[:, :D])).astype(BF)
            result.append(across[which] + jnp.sum(eye * number, axis=0, keepdims=True))
        return tuple(result)

    zero_row = jnp.zeros((1, total), F32)
    across = lax.fori_loop(0, blocks, choose, (zero_row, zero_row))
    srow = lax.broadcasted_iota(jnp.int32, (PAD_SLOTS, total), 0)
    scol = lax.broadcasted_iota(jnp.int32, (PAD_SLOTS, total), 1)
    mine = (scol // PAD_SLOTS == me) & (scol % PAD_SLOTS < slots) & (srow < slots)
    for which in range(2):
        picks[which] = jnp.where(mine & (across[which] == srow.astype(F32) + shift), 1.0, 0.0)
    product[...] = jnp.zeros_like(product)
    square_a[...] = jnp.zeros_like(square_a)
    square_b = zero_row
    good_col = jnp.where(scol[0:1] % PAD_SLOTS < slots, 1.0, 0.0)
    ones = jnp.ones((8, D), F32)
    losses = []
    begin = 0
    for place, end in enumerate(widths):
        cut = slice(begin, end)
        begin = end
        square_b = square_b + exact(ones[:, cut], positives[:, cut].astype(F32) ** 2, NT)[0:1]
        unit_b = lax.rsqrt(square_b + EPS_UNIT)

        def totals(index, carry):
            col_total, loss = carry
            at = pl.ds(start(index), block)
            row, real, eye = masks(index)
            front = anchors[at, cut]
            square_a[at, :] += jnp.sum(front.astype(F32) ** 2, axis=1, keepdims=True)
            product[at, :] += nt(front, positives[:, cut])
            sims = INV_TEMP * lax.rsqrt(square_a[at, :] + EPS_UNIT) * unit_b * product[at, :]
            expo = jnp.where(real, jnp.exp(sims - INV_TEMP), 0.0)
            expos[at, :] = expo
            good = row[:, 0:1] % PAD_SLOTS < slots
            row_total = jnp.where(good, jnp.sum(expo, axis=1, keepdims=True), 1.0)
            row_sum[at, :] = row_total
            row_log = jnp.where(good, INV_TEMP + jnp.log(row_total), 0.0)
            loss = loss + jnp.sum(row_log, axis=0, keepdims=True)
            diag = jnp.sum(jnp.sum(eye * sims, axis=0, keepdims=True), axis=1, keepdims=True)
            return col_total + jnp.sum(expo, axis=0, keepdims=True), loss - 2.0 * diag

        col_total, loss = lax.fori_loop(0, blocks, totals, (zero_row, jnp.zeros((1, 1), F32)))
        col_total = jnp.where(good_col > 0, col_total, 1.0)
        loss = loss + jnp.sum(good_col * (INV_TEMP + jnp.log(col_total)), axis=1, keepdims=True)
        losses.append(loss / (2.0 * slots * (total // PAD_SLOTS)))

        def grads(index, carry):
            pull_a, pull_b, part_b = carry
            at = pl.ds(start(index), block)
            row, real, eye = masks(index)
            unit_a = lax.rsqrt(square_a[at, :] + EPS_UNIT)
            scale = INV_TEMP * unit_a * unit_b
            expo = expos[at, :]
            share = 0.5 * (expo / row_sum[at, :] + expo / col_total) - eye
            toward = share * (scale * product[at, :])
            weight = scale * share
            pull = unit_a * unit_a * jnp.sum(toward, axis=1, keepdims=True)
            pull_a = pull_a + jnp.sum(eye * pull, axis=0, keepdims=True)
            pull_b = pull_b + jnp.sum(toward, axis=0, keepdims=True)
            parts[2 * place, :, at] = exact(picks[1], weight, NT)
            return pull_a, pull_b, part_b + exact(picks[0, :, at], weight, full)

        pull_a, pull_b, part_b = lax.fori_loop(
            0, blocks, grads, (zero_row, zero_row, jnp.zeros((PAD_SLOTS, total), F32)))
        parts[2 * place] = parts[2 * place] - picks[0] * pull_a
        parts[2 * place + 1] = part_b - picks[1] * (unit_b * unit_b * pull_b)
    spans = list(zip((0,) + tuple(widths[:-1]), widths))
    sums[...] = jnp.zeros_like(sums)
    counts = count_ref[:, 0:1]
    for place in range(len(widths) - 1, -1, -1):
        begin, end = spans[place]
        sums[0] += parts[2 * place]
        sums[1] += parts[2 * place + 1]
        grad = exact(sums[0], anchors[:, begin:end].astype(F32), full)
        grad += exact(sums[1], positives[:, begin:end].astype(F32), full)
        grad_ref[:, begin:end] = grad / counts
    lane = lax.broadcasted_iota(jnp.int32, (8, 128), 1)
    out = jnp.zeros((8, 128), F32)
    for place, loss in enumerate(losses):
        out = jnp.where(lane == len(widths) - 1 - place, loss, out)
    loss_ref[...] = out


def contrast(own, other, counts, me, tile, slots):
    widths = (D // 12, D // 6, D // 3, D * 2 // 3, D)
    total = own.shape[0]
    block = min(total, 256)
    whole = lambda shape: pl.BlockSpec(shape, lambda i, *_: (0,) * len(shape))
    return pl.pallas_call(
        functools.partial(contrast_kernel, slots=slots, widths=widths, block=block),
        out_shape=(jax.ShapeDtypeStruct((8, 128), F32), jax.ShapeDtypeStruct((PAD_SLOTS, D), F32)),
        grid_spec=pltpu.PrefetchScalarGridSpec(
            num_scalar_prefetch=1,
            grid=(1,),
            in_specs=[whole((total, own.shape[1])), whole((total, own.shape[1])), whole((PAD_SLOTS, 128))],
            out_specs=[whole((8, 128)), whole((PAD_SLOTS, D))],
            scratch_shapes=[
                pltpu.VMEM((total, D), BF), pltpu.VMEM((total, D), BF),
                pltpu.VMEM((total, total), F32), pltpu.VMEM((total, total), F32),
                pltpu.VMEM((total, 1), F32), pltpu.VMEM((total, 1), F32),
                pltpu.VMEM((2, PAD_SLOTS, total), F32), pltpu.VMEM((2 * len(widths), PAD_SLOTS, total), F32),
                pltpu.VMEM((2, PAD_SLOTS, total), F32)],
        ),
        name="contrast",
    )(jnp.stack([me, tile]).astype(jnp.int32), own, other, counts)


def layer_norm(value, gain, shift):
    center = value - jnp.mean(value, axis=-1, keepdims=True)
    spread = jnp.mean(center * center, axis=-1, keepdims=True)
    return center * lax.rsqrt(spread + EPS_NORM) * gain + shift


def shards(
    layer_input, segment_ids, pad_mask, pair_slots, result_cotangent,
    query_weight, key_weight, value_weight, output_weight,
    query_bias, value_bias, output_bias, first_gain, first_shift,
    inner_weight, inner_bias, outer_weight, outer_bias, second_gain, second_shift,
):
    rows = layer_input.shape[0]
    count, me = lax.axis_size("dp"), lax.axis_index("dp")
    tile = lax.axis_index("tile")
    slots = pair_slots.shape[0]
    own = query_weight.shape[0]
    fold = inner_weight.shape[1] // D
    valid = pad_mask == 1
    vectors = [query_bias, value_bias, output_bias, first_gain, first_shift, outer_bias, second_gain, second_shift]
    columns = jnp.concatenate(
        [v[:, None] for v in vectors] + [inner_bias.reshape(own, fold)]
        + [jnp.zeros((own, 128 - len(vectors) - fold), BF)], axis=1)
    early = gather_rows(jnp.concatenate([query_weight, key_weight, value_weight, columns], axis=1))
    inner_fold = inner_weight.reshape(own, D, fold).transpose(0, 2, 1).reshape(own, fold * D)
    late = lax.all_gather(
        jnp.concatenate([inner_fold, outer_weight.reshape(own, fold * D), output_weight], axis=1),
        ("dp", "tile"), axis=0, tiled=True)
    qkv_full = early[:, :3 * D]
    vec = early[:, 3 * D:].T.astype(F32)
    query_offset, value_offset, output_offset, gain_first, shift_first, outer_offset, gain_second, shift_second = (
        vec[i] for i in range(8))
    inner_offset = vec[8:8 + fold].reshape(fold * D)
    inner_full = late[:, :fold * D]
    outer_full = late[:, fold * D:2 * fold * D].reshape(D, fold, D).transpose(1, 0, 2).reshape(fold * D, D)
    output_full = late[:, 2 * fold * D:]

    keys, queries = mask_codes(segment_ids, valid, slots)
    offset = jnp.concatenate([query_offset, jnp.zeros((D,), F32), value_offset])
    qkv = (dot(layer_input, qkv_full) + offset).astype(BF)
    lo, hi = key_ranges(segment_ids, valid, *FWD_TILES[:2])
    mixed, log_totals = attend_forward(qkv, lo, hi, keys, queries, HEADS, *FWD_TILES)
    branch = dot(mixed, output_full) + output_offset
    hidden, first_back = jax.vjp(layer_norm, layer_input.astype(F32) + branch, gain_first, shift_first)
    hidden_low = hidden.astype(BF)
    inner = dot(hidden_low, inner_full) + inner_offset
    cdf = 0.5 * (1.0 + lax.erf(inner * (0.5 ** 0.5)))
    active = (inner * cdf).astype(BF)
    slope = (cdf + inner * jnp.exp(-0.5 * inner * inner) * 0.3989422804014327).astype(BF)
    outer = dot(active, outer_full) + outer_offset
    result, second_back = jax.vjp(layer_norm, hidden + outer, gain_second, shift_second)

    ids = jnp.arange(PAD_SLOTS, dtype=jnp.int32)
    member = ((segment_ids[None, :] == ids[:, None]) & valid[None, :]).astype(F32)
    counts = jnp.maximum(jnp.sum(member, axis=1, keepdims=True), 1.0)
    pooled = (jnp.dot(member, result, precision=HIGH) / counts).astype(BF)
    numbers = jnp.pad(pair_slots.astype(BF), ((0, PAD_SLOTS - slots), (0, 126)), constant_values=-1)
    packet = jnp.concatenate([pooled, numbers], axis=1)
    packets = lax.all_to_all(jnp.broadcast_to(packet[None], (count,) + packet.shape), "dp", 0, 0, tiled=True)
    packets = packets.reshape(count * PAD_SLOTS, packet.shape[1])
    loss_block, pooled_grad = contrast(
        packets, swap_tile(packets), jnp.broadcast_to(counts, (PAD_SLOTS, 128)), me, tile, slots)
    dim_losses = loss_block[0, :5]
    total_loss = jnp.sum(dim_losses)

    result_grad = result_cotangent.astype(F32) + lax.dot_general(
        member, pooled_grad, TN, precision=HIGH, preferred_element_type=F32)
    norm_grad, second_gain_grad, second_shift_grad = second_back(result_grad)
    outer_grad = norm_grad.astype(BF)
    outer_weight_grad = tn(active, outer_grad)
    outer_bias_grad = jnp.sum(outer_grad, axis=0, dtype=F32)
    inner_grad = (nt(outer_grad, outer_full) * slope.astype(F32)).astype(BF)
    inner_weight_grad = tn(hidden_low, inner_grad)
    inner_bias_grad = jnp.sum(inner_grad, axis=0, dtype=F32)
    feed = jnp.concatenate(
        [inner_weight_grad.astype(BF),
         outer_weight_grad.astype(BF).reshape(fold, D, D).transpose(1, 0, 2).reshape(D, fold * D)], axis=1)
    feed_shard = lax.psum_scatter(feed, ("dp", "tile"), scatter_dimension=0, tiled=True).astype(F32)
    hidden_grad = norm_grad + nt(inner_grad, inner_full)

    residual_grad, first_gain_grad, first_shift_grad = first_back(hidden_grad)
    branch_grad = residual_grad.astype(BF)
    output_weight_grad = tn(mixed, branch_grad)
    output_bias_grad = jnp.sum(branch_grad, axis=0, dtype=F32)
    mixed_grad = nt(branch_grad, output_full).astype(BF)
    lo, hi = key_ranges(segment_ids, valid, *BWD_TILES[:2])
    query_grad, key_grad, value_grad = attend_backward(
        qkv, mixed_grad, mixed, log_totals.reshape(-1, 2 * BWD_TILES[2], rows), lo, hi, keys, queries, HEADS, *BWD_TILES)
    vector_grads = jnp.stack(
        [jnp.sum(query_grad, axis=0, dtype=F32), jnp.sum(value_grad, axis=0, dtype=F32), output_bias_grad,
         first_gain_grad, first_shift_grad, outer_bias_grad, second_gain_grad, second_shift_grad]
        + [inner_bias_grad[i * D:(i + 1) * D] for i in range(fold)], axis=0)
    vector_grads = jnp.pad(vector_grads, ((0, 128 - vector_grads.shape[0]), (0, 0))).T
    attention_grads = jnp.concatenate(
        [tn(layer_input, query_grad).astype(BF), tn(layer_input, key_grad).astype(BF),
         tn(layer_input, value_grad).astype(BF), output_weight_grad.astype(BF), vector_grads.astype(BF)], axis=1)
    shard = scatter_rows(attention_grads)
    input_grad = (
        residual_grad + nt(query_grad, qkv_full[:, :D]) + nt(key_grad, qkv_full[:, D:2 * D])
        + nt(value_grad, qkv_full[:, 2 * D:]))
    small = shard[:, 4 * D:].T
    return (
        total_loss, dim_losses, result.astype(BF), input_grad,
        shard[:, :D], shard[:, D:2 * D], shard[:, 2 * D:3 * D], shard[:, 3 * D:4 * D],
        small[0], small[1], small[2], small[3], small[4],
        feed_shard[:, :fold * D].reshape(own, fold, D).transpose(0, 2, 1).reshape(own, fold * D),
        small[8:8 + fold].T.reshape(own * fold),
        feed_shard[:, fold * D:].reshape(own * fold, D),
        small[5], small[6], small[7],
    )


def solution(mesh):
    both = ("dp", "tile")
    wide, flat = P(both, None), P(both)
    return jax.shard_map(
        shards,
        mesh=mesh,
        in_specs=(wide, flat, flat, P("dp", None), wide, wide, wide, wide, wide)
        + (flat,) * 5 + (wide, flat, wide) + (flat,) * 3,
        out_specs=(P(), P(), wide, wide, wide, wide, wide, wide) + (flat,) * 5 + (wide, flat, wide) + (flat,) * 3,
        check_vma=False,
    )
```

```python
import functools

import jax
import jax.numpy as jnp
from jax import lax
from jax.experimental import pallas as pl
from jax.experimental.pallas import tpu as pltpu
from jax.sharding import PartitionSpec as P

D = 768
HEADS = 12
HEAD_DIM = 64
EPS_NORM = 1e-12
EPS_UNIT = 1e-06
INV_TEMP = 20.0
NEG_FILL = -1e30
HIGH = lax.Precision.HIGHEST
F32 = jnp.float32
BF = jnp.bfloat16
NT = (((1,), (1,)), ((), ()))
TN = (((0,), (0,)), ((), ()))
FWD_TILES = (256, 256, 6)
BWD_TILES = (256, 256, 6)
PAD_SLOTS = 16


def dot(a, b):
    return jnp.dot(a, b, preferred_element_type=F32)


def nt(a, b):
    return lax.dot_general(a, b, NT, preferred_element_type=F32)


def tn(a, b):
    return lax.dot_general(a, b, TN, preferred_element_type=F32)


def digits_of(count):
    digits, stride = [], 1
    while count > 1:
        radix = 4 if count % 4 == 0 else (2 if count % 2 == 0 else count)
        digits.append((stride, radix))
        stride, count = stride * radix, count // radix
    return digits


def peer(index, stride, radix, step):
    digit = index // stride % radix
    other = digit ^ step if radix in (2, 4) else (digit + step) % radix
    return index + (other - digit) * stride


def back(index, stride, radix, step):
    digit = index // stride % radix
    other = digit ^ step if radix in (2, 4) else (digit - step) % radix
    return index + (other - digit) * stride


def send_to(value, count, stride, radix, step):
    return lax.ppermute(value, "dp", [(i, peer(i, stride, radix, step)) for i in range(count)])


def swap_tile(value):
    return lax.ppermute(value, "tile", [(0, 1), (1, 0)])


def gather_pieces(shard):
    count, me = lax.axis_size("dp"), lax.axis_index("dp")
    stack, sources = shard[None], [me]
    digits = digits_of(count)[::-1]
    for level, (stride, radix) in enumerate(digits):
        stacks, origins = [stack], [sources]
        for step in range(1, radix):
            stacks.append(send_to(stack, count, stride, radix, step))
            origins.append([back(source, stride, radix, step) for source in sources])
        if level == len(digits) - 1:
            return stacks, origins
        stack, sources = jnp.concatenate(stacks, axis=0), sum(origins, [])
    return [stack], [sources]


def place_kernel(slots, *refs, sizes):
    count = len(sizes)
    pieces, out, sems = refs[:count], refs[count], refs[count + 1]
    copies, number = [], 0
    for piece, size in zip(pieces, sizes):
        for entry in range(size):
            copies.append(pltpu.make_async_copy(piece.at[entry], out.at[slots[number]], sems.at[number]))
            number += 1
    for copy in copies:
        copy.start()
    for copy in copies:
        copy.wait()


def gather_rows(shard):
    stacks, origins = gather_pieces(shard)
    tile = lax.axis_index("tile")
    others = [swap_tile(stack) for stack in stacks]
    slots = [origin * 2 + tile for group in origins for origin in group]
    slots += [origin * 2 + (1 - tile) for group in origins for origin in group]
    sizes = [stack.shape[0] for stack in stacks] * 2
    total = sum(sizes)
    placed = pl.pallas_call(
        functools.partial(place_kernel, sizes=sizes),
        out_shape=jax.ShapeDtypeStruct((total,) + shard.shape, shard.dtype),
        grid_spec=pltpu.PrefetchScalarGridSpec(
            num_scalar_prefetch=1,
            grid=(1,),
            in_specs=[pl.BlockSpec(memory_space=pl.ANY)] * len(sizes),
            out_specs=pl.BlockSpec((total,) + shard.shape, lambda i, *_: (0, 0, 0)),
            scratch_shapes=[pltpu.SemaphoreType.DMA((total,))],
        ),
        name="place_rows",
    )(jnp.stack(slots).astype(jnp.int32), *stacks, *others)
    return placed.reshape(total * shard.shape[0], shard.shape[1])


def take(value, index, axis):
    return lax.dynamic_index_in_dim(value, index, axis, keepdims=False)


def scatter_rows(partial):
    count, me = lax.axis_size("dp"), lax.axis_index("dp")
    tile = lax.axis_index("tile")
    rows = partial.shape[0] // (2 * count)
    blocks = partial.reshape(count, 2, rows, partial.shape[1])
    got = swap_tile(take(blocks, 1 - tile, 1))
    total = take(blocks, tile, 1).astype(F32) + got.astype(F32)
    for stride, radix in digits_of(count):
        total = total.astype(BF).reshape(-1, radix, rows, partial.shape[1])
        digit = me // stride % radix
        sent = []
        for step in range(1, radix):
            other = peer(me, stride, radix, step) // stride % radix
            sent.append(send_to(take(total, other, 1), count, stride, radix, step))
        total = take(total, digit, 1).astype(F32)
        for value in sent:
            total = total + value.astype(F32)
    return total.reshape(rows, partial.shape[1])


def key_ranges(segment_ids, valid, tq, tk):
    rows = segment_ids.shape[0]
    tiles = segment_ids.reshape(rows // tq, tq)
    first, last = tiles[:, 0], tiles[:, -1]
    lo = jnp.sum((segment_ids[None, :] < first[:, None]).astype(jnp.int32), axis=1)
    hi = jnp.sum(((segment_ids[None, :] <= last[:, None]) & valid[None, :]).astype(jnp.int32), axis=1)
    return lo // tk, (hi + tk - 1) // tk


def mask_codes(segment_ids, valid, slots):
    half = 64
    ids = jnp.arange(half, dtype=jnp.int32)
    code = jnp.where(valid, segment_ids, slots)
    keys = (code[:, None] == ids[None, :]).astype(BF)
    block = (segment_ids[None, :] != ids[:, None]) & (ids[:, None] <= slots)
    queries = jnp.where(block, NEG_FILL, 0.0).astype(BF)
    return keys, queries


def fwd_kernel(lo_ref, hi_ref, q_ref, k_ref, v_ref, kc_ref, qc_ref, o_ref, lse_ref, kaug, vt, scores, *, tq, tk):
    rows = q_ref.shape[0]
    nh = q_ref.shape[1] // 64
    kc = kc_ref[...]
    k = k_ref[...]
    for h in range(nh):
        kaug[h] = jnp.concatenate([k[:, 64 * h:64 * h + 64], kc], axis=1)
    vt[...] = v_ref[...].T

    def q_step(i, _):
        q0 = pl.multiple_of(i * tq, tq)
        qt = (q_ref[pl.ds(q0, tq), :] * jnp.asarray(0.125, BF)).T
        qc = qc_ref[:, pl.ds(q0, tq)]
        qa = [jnp.concatenate([qt[64 * h:64 * h + 64], qc], axis=0) for h in range(nh)]

        def score_step(j, tops):
            k0 = pl.multiple_of(j * tk, tk)
            result = []
            for h in range(nh):
                s = dot(kaug[h, pl.ds(k0, tk), :], qa[h])
                scores[h, pl.ds(k0, tk), :] = s
                result.append(jnp.maximum(tops[h], jnp.max(s.reshape(tk // 8, 8, tq), axis=0)))
            return tuple(result)

        tops = lax.fori_loop(lo_ref[i], hi_ref[i], score_step, tuple(jnp.full((8, tq), NEG_FILL, F32) for _ in range(nh)))
        peak = [jnp.max(top, axis=0, keepdims=True) for top in tops]

        def mix_step(j, carry):
            k0 = pl.multiple_of(j * tk, tk)
            probs, result = [], []
            for h in range(nh + 1):
                if h < nh:
                    p = jnp.exp(scores[h, pl.ds(k0, tk), :] - peak[h])
                    total = carry[h][0] + jnp.sum(p.reshape(tk // 8, 8, tq), axis=0)
                    probs.append((total, p.astype(BF)))
                if h >= 1:
                    total, p = probs[h - 1]
                    acc = carry[h - 1][1] + dot(vt[64 * (h - 1):64 * h, pl.ds(k0, tk)], p)
                    result.append((total, acc))
            return tuple(result)

        init = tuple((jnp.zeros((8, tq), F32), jnp.zeros((64, tq), F32)) for _ in range(nh))
        res = lax.fori_loop(lo_ref[i], hi_ref[i], mix_step, init)
        outs = []
        for h in range(nh):
            total, acc = res[h]
            total = jnp.sum(total, axis=0, keepdims=True)
            outs.append(acc / total)
            lse_ref[0, h:h + 1, pl.ds(q0, tq)] = peak[h] + jnp.log(total)
        o_ref[pl.ds(q0, tq), :] = jnp.concatenate(outs, axis=0).T.astype(BF)
        return 0

    lax.fori_loop(0, rows // tq, q_step, 0)


def attend_forward(qkv, lo, hi, keys, queries, heads, tq, tk, hp):
    rows = qkv.shape[0]
    pairs = heads // 2
    steps = pairs // hp
    col = lambda off: pl.BlockSpec((rows, 128 * hp), lambda h, *_: (0, off + h))
    return pl.pallas_call(
        functools.partial(fwd_kernel, tq=tq, tk=tk),
        out_shape=(jax.ShapeDtypeStruct((rows, heads * 64), BF), jax.ShapeDtypeStruct((steps, 2 * hp, rows), F32)),
        grid_spec=pltpu.PrefetchScalarGridSpec(
            num_scalar_prefetch=2,
            grid=(steps,),
            in_specs=[col(0), col(steps), col(2 * steps),
                      pl.BlockSpec((rows, 64), lambda h, *_: (0, 0)),
                      pl.BlockSpec((64, rows), lambda h, *_: (0, 0))],
            out_specs=[pl.BlockSpec((rows, 128 * hp), lambda h, *_: (0, h)),
                       pl.BlockSpec((1, 2 * hp, rows), lambda h, *_: (h, 0, 0))],
            scratch_shapes=[pltpu.VMEM((2 * hp, rows, 128), BF), pltpu.VMEM((128 * hp, rows), BF),
                            pltpu.VMEM((2 * hp, rows, tq), F32)],
        ),
        name="attend_forward",
    )(lo, hi, qkv, qkv, qkv, keys, queries)


def bwd_kernel(lo_ref, hi_ref, q_ref, k_ref, v_ref, g_ref, o_ref, lse_ref, kc_ref, qc_ref,
               dq_ref, dk_ref, dv_ref, kaug, kt, dk, dv, *, tq, tk):
    rows = q_ref.shape[0]
    nh = q_ref.shape[1] // 64
    kc = kc_ref[...]
    k = k_ref[...]
    for h in range(nh):
        kaug[h] = jnp.concatenate([k[:, 64 * h:64 * h + 64], kc], axis=1)
    kt[...] = k.T
    dk[...] = jnp.zeros_like(dk)
    dv[...] = jnp.zeros_like(dv)
    lane = lax.broadcasted_iota(jnp.int32, (tq, 128), 1)
    sub = lax.broadcasted_iota(jnp.int32, (128, tq), 0)

    def q_step(i, _):
        q0 = pl.multiple_of(i * tq, tq)
        q = q_ref[pl.ds(q0, tq), :] * jnp.asarray(0.125, BF)
        g = g_ref[pl.ds(q0, tq), :]
        qt = q.T
        gt = g.T
        prod = gt.astype(F32) * o_ref[pl.ds(q0, tq), :].T.astype(F32)
        qc = qc_ref[:, pl.ds(q0, tq)]
        zero = jnp.zeros((), BF)
        qa, ga, delta, lse = [], [], [], []
        for h in range(nh):
            qa.append(jnp.concatenate([qt[64 * h:64 * h + 64], qc], axis=0))
            gp = gt[128 * (h // 2):128 * (h // 2) + 128]
            ga.append(jnp.where(sub // 64 == h % 2, gp, zero))
            delta.append(jnp.sum(prod[64 * h:64 * h + 64], axis=0, keepdims=True))
            lse.append(lse_ref[0, h:h + 1, pl.ds(q0, tq)])
        qz = [jnp.concatenate([jnp.where(lane // 64 == h, q[:, 128 * w:128 * w + 128], zero) for h in range(2)], axis=0) for w in range(nh // 2)]
        gz = [jnp.concatenate([jnp.where(lane // 64 == h, g[:, 128 * w:128 * w + 128], zero) for h in range(2)], axis=0) for w in range(nh // 2)]

        def k_step(j, carry):
            k0 = pl.multiple_of(j * tk, tk)
            v = v_ref[pl.ds(k0, tk), :]
            ps, dss, dqs, first = [], [], [], []
            for h in range(nh + 2):
                if h < nh:
                    first.append((dot(kaug[h, pl.ds(k0, tk), :], qa[h]),
                                  dot(v[:, 128 * (h // 2):128 * (h // 2) + 128], ga[h])))
                if 1 <= h <= nh:
                    s, dp = first[h - 1]
                    p = jnp.exp(s - lse[h - 1])
                    dss.append((p * (dp - delta[h - 1])).astype(BF))
                    ps.append(p.astype(BF))
                if h >= 2:
                    g = h - 2
                    dqs.append(carry[g] + dot(kt[64 * g:64 * g + 64, pl.ds(k0, tk)], dss[g]))
                    if g % 2 == 1:
                        w = g // 2
                        at = slice(128 * w, 128 * w + 128)
                        dv[pl.ds(k0, tk), at] += dot(jnp.concatenate(ps[g - 1:g + 1], axis=1), gz[w])
                        dk[pl.ds(k0, tk), at] += dot(jnp.concatenate(dss[g - 1:g + 1], axis=1), qz[w])
            return tuple(dqs)

        res = lax.fori_loop(lo_ref[i], hi_ref[i], k_step, tuple(jnp.zeros((64, tq), F32) for _ in range(nh)))
        dq_ref[pl.ds(q0, tq), :] = (jnp.concatenate(res, axis=0) * 0.125).T.astype(BF)
        return 0

    lax.fori_loop(0, rows // tq, q_step, 0)
    dk_ref[...] = dk[...].astype(BF)
    dv_ref[...] = dv[...].astype(BF)


def attend_backward(qkv, grad, mixed, lse, lo, hi, keys, queries, heads, tq, tk, hp):
    rows = qkv.shape[0]
    pairs = heads // 2
    steps = pairs // hp
    col = lambda off: pl.BlockSpec((rows, 128 * hp), lambda h, *_: (0, off + h))
    sd = jax.ShapeDtypeStruct((rows, heads * 64), BF)
    return pl.pallas_call(
        functools.partial(bwd_kernel, tq=tq, tk=tk),
        out_shape=(sd, sd, sd),
        grid_spec=pltpu.PrefetchScalarGridSpec(
            num_scalar_prefetch=2,
            grid=(steps,),
            in_specs=[col(0), col(steps), col(2 * steps), col(0), col(0),
                      pl.BlockSpec((1, 2 * hp, rows), lambda h, *_: (h, 0, 0)),
                      pl.BlockSpec((rows, 64), lambda h, *_: (0, 0)),
                      pl.BlockSpec((64, rows), lambda h, *_: (0, 0))],
            out_specs=[pl.BlockSpec((rows, 128 * hp), lambda h, *_: (0, h))] * 3,
            scratch_shapes=[pltpu.VMEM((2 * hp, rows, 128), BF), pltpu.VMEM((128 * hp, rows), BF),
                            pltpu.VMEM((rows, 128 * hp), F32), pltpu.VMEM((rows, 128 * hp), F32)],
        ),
        name="attend_backward",
    )(lo, hi, qkv, qkv, qkv, grad, mixed, lse, keys, queries)


def exact(a, b, dims):
    return lax.dot_general(a, b, dims, precision=HIGH, preferred_element_type=F32)


def contrast_kernel(
    place_ref, own_ref, other_ref, count_ref, loss_ref, grad_ref,
    anchors, positives, product, expos, square_a, row_sum, picks, parts, sums, *, slots, widths, block,
):
    me, tile = place_ref[0], place_ref[1]
    total = own_ref.shape[0]
    blocks = total // block
    full = (((1,), (0,)), ((), ()))
    col = lax.broadcasted_iota(jnp.int32, (block, total), 1)
    base = lax.broadcasted_iota(jnp.int32, (block, total), 0)
    shift = slots * tile.astype(F32)
    away = slots * (1 - tile).astype(F32)

    def masks(index):
        row = base + index * block
        real = (row % PAD_SLOTS < slots) & (col % PAD_SLOTS < slots)
        return row, real, jnp.where((row == col) & real, 1.0, 0.0)

    def start(index):
        return pl.multiple_of(index * block, block)

    def choose(index, across):
        at = pl.ds(start(index), block)
        row, real, eye = masks(index)
        numbers = own_ref[at, D:].astype(F32)
        local = (col % PAD_SLOTS).astype(F32)
        ok = (row // PAD_SLOTS == col // PAD_SLOTS) & real
        result = []
        for which, chosen in enumerate((anchors, positives)):
            number = numbers[:, which:which + 1]
            near_own = jnp.where(ok & (number == local + shift), 1.0, 0.0).astype(BF)
            near_other = jnp.where(ok & (number == local + away), 1.0, 0.0).astype(BF)
            chosen[at, :] = (dot(near_own, own_ref[:, :D]) + dot(near_other, other_ref[:, :D])).astype(BF)
            result.append(across[which] + jnp.sum(eye * number, axis=0, keepdims=True))
        return tuple(result)

    zero_row = jnp.zeros((1, total), F32)
    across = lax.fori_loop(0, blocks, choose, (zero_row, zero_row))
    srow = lax.broadcasted_iota(jnp.int32, (PAD_SLOTS, total), 0)
    scol = lax.broadcasted_iota(jnp.int32, (PAD_SLOTS, total), 1)
    mine = (scol // PAD_SLOTS == me) & (scol % PAD_SLOTS < slots) & (srow < slots)
    for which in range(2):
        picks[which] = jnp.where(mine & (across[which] == srow.astype(F32) + shift), 1.0, 0.0)
    product[...] = jnp.zeros_like(product)
    square_a[...] = jnp.zeros_like(square_a)
    square_b = zero_row
    good_col = jnp.where(scol[0:1] % PAD_SLOTS < slots, 1.0, 0.0)
    ones = jnp.ones((8, D), F32)
    losses = []
    begin = 0
    for place, end in enumerate(widths):
        cut = slice(begin, end)
        begin = end
        square_b = square_b + exact(ones[:, cut], positives[:, cut].astype(F32) ** 2, NT)[0:1]
        unit_b = lax.rsqrt(square_b + EPS_UNIT)

        def totals(index, carry):
            col_total, loss = carry
            at = pl.ds(start(index), block)
            row, real, eye = masks(index)
            front = anchors[at, cut]
            square_a[at, :] += jnp.sum(front.astype(F32) ** 2, axis=1, keepdims=True)
            product[at, :] += nt(front, positives[:, cut])
            sims = INV_TEMP * lax.rsqrt(square_a[at, :] + EPS_UNIT) * unit_b * product[at, :]
            expo = jnp.where(real, jnp.exp(sims - INV_TEMP), 0.0)
            expos[at, :] = expo
            good = row[:, 0:1] % PAD_SLOTS < slots
            row_total = jnp.where(good, jnp.sum(expo, axis=1, keepdims=True), 1.0)
            row_sum[at, :] = row_total
            row_log = jnp.where(good, INV_TEMP + jnp.log(row_total), 0.0)
            loss = loss + jnp.sum(row_log, axis=0, keepdims=True)
            diag = jnp.sum(jnp.sum(eye * sims, axis=0, keepdims=True), axis=1, keepdims=True)
            return col_total + jnp.sum(expo, axis=0, keepdims=True), loss - 2.0 * diag

        col_total, loss = lax.fori_loop(0, blocks, totals, (zero_row, jnp.zeros((1, 1), F32)))
        col_total = jnp.where(good_col > 0, col_total, 1.0)
        loss = loss + jnp.sum(good_col * (INV_TEMP + jnp.log(col_total)), axis=1, keepdims=True)
        losses.append(loss / (2.0 * slots * (total // PAD_SLOTS)))

        def grads(index, carry):
            pull_a, pull_b, part_b = carry
            at = pl.ds(start(index), block)
            row, real, eye = masks(index)
            unit_a = lax.rsqrt(square_a[at, :] + EPS_UNIT)
            scale = INV_TEMP * unit_a * unit_b
            expo = expos[at, :]
            share = 0.5 * (expo / row_sum[at, :] + expo / col_total) - eye
            toward = share * (scale * product[at, :])
            weight = scale * share
            pull = unit_a * unit_a * jnp.sum(toward, axis=1, keepdims=True)
            pull_a = pull_a + jnp.sum(eye * pull, axis=0, keepdims=True)
            pull_b = pull_b + jnp.sum(toward, axis=0, keepdims=True)
            parts[2 * place, :, at] = exact(picks[1], weight, NT)
            return pull_a, pull_b, part_b + exact(picks[0, :, at], weight, full)

        pull_a, pull_b, part_b = lax.fori_loop(
            0, blocks, grads, (zero_row, zero_row, jnp.zeros((PAD_SLOTS, total), F32)))
        parts[2 * place] = parts[2 * place] - picks[0] * pull_a
        parts[2 * place + 1] = part_b - picks[1] * (unit_b * unit_b * pull_b)
    spans = list(zip((0,) + tuple(widths[:-1]), widths))
    sums[...] = jnp.zeros_like(sums)
    counts = count_ref[:, 0:1]
    for place in range(len(widths) - 1, -1, -1):
        begin, end = spans[place]
        sums[0] += parts[2 * place]
        sums[1] += parts[2 * place + 1]
        grad = exact(sums[0], anchors[:, begin:end].astype(F32), full)
        grad += exact(sums[1], positives[:, begin:end].astype(F32), full)
        grad_ref[:, begin:end] = grad / counts
    lane = lax.broadcasted_iota(jnp.int32, (8, 128), 1)
    out = jnp.zeros((8, 128), F32)
    for place, loss in enumerate(losses):
        out = jnp.where(lane == len(widths) - 1 - place, loss, out)
    loss_ref[...] = out


def contrast(own, other, counts, me, tile, slots):
    widths = (D // 12, D // 6, D // 3, D * 2 // 3, D)
    total = own.shape[0]
    block = min(total, 256)
    whole = lambda shape: pl.BlockSpec(shape, lambda i, *_: (0,) * len(shape))
    return pl.pallas_call(
        functools.partial(contrast_kernel, slots=slots, widths=widths, block=block),
        out_shape=(jax.ShapeDtypeStruct((8, 128), F32), jax.ShapeDtypeStruct((PAD_SLOTS, D), F32)),
        grid_spec=pltpu.PrefetchScalarGridSpec(
            num_scalar_prefetch=1,
            grid=(1,),
            in_specs=[whole((total, own.shape[1])), whole((total, own.shape[1])), whole((PAD_SLOTS, 128))],
            out_specs=[whole((8, 128)), whole((PAD_SLOTS, D))],
            scratch_shapes=[
                pltpu.VMEM((total, D), BF), pltpu.VMEM((total, D), BF),
                pltpu.VMEM((total, total), F32), pltpu.VMEM((total, total), F32),
                pltpu.VMEM((total, 1), F32), pltpu.VMEM((total, 1), F32),
                pltpu.VMEM((2, PAD_SLOTS, total), F32), pltpu.VMEM((2 * len(widths), PAD_SLOTS, total), F32),
                pltpu.VMEM((2, PAD_SLOTS, total), F32)],
        ),
        name="contrast",
    )(jnp.stack([me, tile]).astype(jnp.int32), own, other, counts)


ROOT_HALF = 0.5 ** 0.5
DENSITY = 0.3989422804014327


def norm_parts(value):
    center = value - jnp.mean(value, axis=1, keepdims=True)
    factor = lax.rsqrt(jnp.mean(center * center, axis=1, keepdims=True) + EPS_NORM)
    return center * factor, factor


def norm_back(grad, gain, normed, factor):
    scaled = grad * gain
    along = jnp.mean(scaled * normed, axis=1, keepdims=True)
    return factor * (scaled - jnp.mean(scaled, axis=1, keepdims=True) - normed * along)


def split(value, terms):
    result = []
    for _ in range(terms - 1):
        low = value.astype(BF)
        result.append(low)
        value = value - low.astype(F32)
    return result + [value.astype(BF)]


def membership(code, count):
    ids = lax.broadcasted_iota(jnp.int32, (PAD_SLOTS, count), 0)
    return jnp.where(ids == code, 1.0, 0.0)


def feed_forward_kernel(
    mixed_ref, x_ref, code_ref, number_ref, vec_ref, late_ref,
    low_ref, first_ref, second_ref, active_ref, slope_ref, out_ref, packet_ref, count_ref, pooled, counts, *, fold,
):
    step = pl.program_id(0)
    vec = lambda i: vec_ref[i:i + 1, :]

    @pl.when(step == 0)
    def _():
        pooled[...] = jnp.zeros_like(pooled)
        counts[...] = jnp.zeros_like(counts)

    total = x_ref[...].astype(F32) + dot(mixed_ref[...], late_ref[:, 2 * fold * D:]) + vec(2)
    first_ref[...] = total
    hidden = norm_parts(total)[0] * vec(3) + vec(4)
    low = hidden.astype(BF)
    low_ref[...] = low
    outer = hidden + vec(5)
    actives = []
    for j in range(fold + 1):
        if j < fold:
            at = slice(j * D, (j + 1) * D)
            inner = dot(low, late_ref[:, at]) + vec(8 + j)
            cdf = 0.5 + 0.5 * lax.erf(inner * ROOT_HALF)
            active = (inner * cdf).astype(BF)
            active_ref[:, at] = active
            slope_ref[:, at] = (cdf + inner * (jnp.exp(-0.5 * inner * inner) * DENSITY)).astype(BF)
            actives.append(active)
        if j >= 1:
            outer += dot(actives[j - 1], late_ref[:, (fold + j - 1) * D:(fold + j) * D])
    second_ref[...] = outer
    result = norm_parts(outer)[0] * vec(6) + vec(7)
    out_ref[...] = result.astype(BF)
    member = membership(code_ref[...], result.shape[0])
    high, rest = split(result, 2)
    pooled[...] += dot(member.astype(BF), high) + dot(member.astype(BF), rest)
    counts[...] += jnp.sum(member, axis=1, keepdims=True)

    @pl.when(step == pl.num_programs(0) - 1)
    def _():
        safe = jnp.maximum(counts[...], 1.0)
        packet = jnp.concatenate([(pooled[...] / safe[:, 0:1]).astype(BF), number_ref[...]], axis=1)
        packet_ref[...] = jnp.broadcast_to(packet[None], packet_ref.shape)
        count_ref[...] = safe


def feed_forward(mixed, x, code, numbers, vec, late, count, fold):
    rows = x.shape[0]
    block = 256
    by_row = lambda width: pl.BlockSpec((block, width), lambda i: (i, 0))
    whole = lambda shape: pl.BlockSpec(shape, lambda i: (0,) * len(shape))
    shape = jax.ShapeDtypeStruct
    packet = (count, PAD_SLOTS, D + 128)
    return pl.pallas_call(
        functools.partial(feed_forward_kernel, fold=fold),
        grid=(rows // block,),
        in_specs=[by_row(D), by_row(D), pl.BlockSpec((1, block), lambda i: (0, i)), whole((PAD_SLOTS, 128)),
                  whole(vec.shape),
                  pl.BlockSpec(late.shape, lambda i: (0, 0), pipeline_mode=pl.Buffered(1))],
        out_specs=[by_row(D), by_row(D), by_row(D), by_row(fold * D), by_row(fold * D), by_row(D),
                   whole(packet), whole((PAD_SLOTS, 128))],
        out_shape=[shape((rows, D), BF), shape((rows, D), F32), shape((rows, D), F32), shape((rows, fold * D), BF),
                   shape((rows, fold * D), BF), shape((rows, D), BF), shape(packet, BF), shape((PAD_SLOTS, 128), F32)],
        scratch_shapes=[pltpu.VMEM((PAD_SLOTS, D), F32), pltpu.VMEM((PAD_SLOTS, 128), F32)],
        cost_estimate=pl.CostEstimate(
            flops=2 * rows * D * D * (2 * fold + 1), bytes_accessed=late.size * 2 + rows * D * 36, transcendentals=0),
        compiler_params=pltpu.CompilerParams(vmem_limit_bytes=60 * 2 ** 20),
        name="feed_forward",
    )(mixed, x, code, numbers, vec, late)


def feed_backward_kernel(
    cot_ref, code_ref, pooled_ref, vec_ref, first_ref, second_ref, slope_ref, late_ref,
    outer_ref, inner_ref, residual_ref, branch_ref, mixed_ref, sums_ref, *, fold,
):
    @pl.when(pl.program_id(0) == 0)
    def _():
        sums_ref[...] = jnp.zeros_like(sums_ref)

    vec = lambda i: vec_ref[i:i + 1, :]

    def add(i, value):
        sums_ref[i:i + 1, :] += jnp.sum(value, axis=0, keepdims=True)

    count = cot_ref.shape[0]
    member = membership(code_ref[...], count).astype(BF)
    spread = tn(jnp.concatenate([member] * 3, axis=0), jnp.concatenate(split(pooled_ref[...], 3), axis=0))
    grad = cot_ref[...].astype(F32) + spread
    normed, factor = norm_parts(second_ref[...])
    add(6, grad * normed)
    add(7, grad)
    grad = norm_back(grad, vec(6), normed, factor)
    outer = grad.astype(BF)
    outer_ref[...] = outer
    add(5, outer.astype(F32))
    inners = []
    for j in range(fold + 1):
        if j < fold:
            at = slice(j * D, (j + 1) * D)
            inner = (nt(outer, late_ref[:, (fold + j) * D:(fold + j + 1) * D]) * slope_ref[:, at].astype(F32)).astype(BF)
            inner_ref[:, at] = inner
            add(8 + j, inner.astype(F32))
            inners.append(inner)
        if j >= 1:
            grad += nt(inners[j - 1], late_ref[:, (j - 1) * D:j * D])
    normed, factor = norm_parts(first_ref[...])
    add(3, grad * normed)
    add(4, grad)
    grad = norm_back(grad, vec(3), normed, factor)
    residual_ref[...] = grad
    branch = grad.astype(BF)
    branch_ref[...] = branch
    add(2, branch.astype(F32))
    mixed_ref[...] = nt(branch, late_ref[:, 2 * fold * D:]).astype(BF)


def feed_backward(cot, code, pooled_grad, vec, first, second, slope, late, fold):
    rows = cot.shape[0]
    block = 256
    by_row = lambda width: pl.BlockSpec((block, width), lambda i: (i, 0))
    whole = lambda shape: pl.BlockSpec(shape, lambda i: (0,) * len(shape))
    shape = jax.ShapeDtypeStruct
    return pl.pallas_call(
        functools.partial(feed_backward_kernel, fold=fold),
        grid=(rows // block,),
        in_specs=[by_row(D), pl.BlockSpec((1, block), lambda i: (0, i)), whole((PAD_SLOTS, D)), whole(vec.shape),
                  by_row(D), by_row(D), by_row(fold * D),
                  pl.BlockSpec(late.shape, lambda i: (0, 0), pipeline_mode=pl.Buffered(1))],
        out_specs=[by_row(D), by_row(fold * D), by_row(D), by_row(D), by_row(D), whole((16, D))],
        out_shape=[shape((rows, D), BF), shape((rows, fold * D), BF), shape((rows, D), F32), shape((rows, D), BF),
                   shape((rows, D), BF), shape((16, D), F32)],
        cost_estimate=pl.CostEstimate(
            flops=2 * rows * D * D * (2 * fold + 1), bytes_accessed=late.size * 2 + rows * D * 34, transcendentals=0),
        compiler_params=pltpu.CompilerParams(vmem_limit_bytes=60 * 2 ** 20),
        name="feed_backward",
    )(cot, code, pooled_grad, vec, first, second, slope, late)


def feed_weights_kernel(low_ref, inner_ref, active_ref, outer_ref, out_ref, *, fold):
    step = pl.program_id(0)

    @pl.when(step < fold)
    def _():
        out_ref[...] = tn(low_ref[...], inner_ref[...]).astype(BF)

    @pl.when(step >= fold)
    def _():
        out_ref[...] = tn(active_ref[...], outer_ref[...]).astype(BF)


def feed_weights(low, inner, active, outer, fold):
    rows = low.shape[0]
    col = lambda f: pl.BlockSpec((rows, D), lambda j: (0, f(j)))
    return pl.pallas_call(
        functools.partial(feed_weights_kernel, fold=fold),
        grid=(2 * fold,),
        in_specs=[col(lambda j: 0), col(lambda j: jnp.minimum(j, fold - 1)), col(lambda j: jnp.maximum(j - fold, 0)),
                  col(lambda j: 0)],
        out_specs=pl.BlockSpec((D, D), lambda j: (0, j)),
        out_shape=jax.ShapeDtypeStruct((D, 2 * fold * D), BF),
        cost_estimate=pl.CostEstimate(
            flops=4 * fold * rows * D * D, bytes_accessed=4 * rows * D * (fold + 1) + 4 * fold * D * D,
            transcendentals=0),
        compiler_params=pltpu.CompilerParams(vmem_limit_bytes=60 * 2 ** 20),
        name="feed_weights",
    )(low, inner, active, outer)


def shards(
    layer_input, segment_ids, pad_mask, pair_slots, result_cotangent,
    query_weight, key_weight, value_weight, output_weight,
    query_bias, value_bias, output_bias, first_gain, first_shift,
    inner_weight, inner_bias, outer_weight, outer_bias, second_gain, second_shift,
):
    rows = layer_input.shape[0]
    count, me = lax.axis_size("dp"), lax.axis_index("dp")
    tile = lax.axis_index("tile")
    slots = pair_slots.shape[0]
    own = query_weight.shape[0]
    fold = inner_weight.shape[1] // D
    valid = pad_mask == 1
    flat = jnp.concatenate(
        [query_bias, value_bias, output_bias, first_gain, first_shift, outer_bias, second_gain, second_shift,
         inner_bias.reshape(own, fold).T.reshape(-1)])
    flat = jnp.pad(flat, (0, 3 * D - flat.shape[0]))
    early = gather_rows(jnp.concatenate(
        [jnp.concatenate([query_weight, key_weight, value_weight], axis=1), jnp.broadcast_to(flat[None], (8, 3 * D))],
        axis=0))
    inner_fold = inner_weight.reshape(own, D, fold).transpose(0, 2, 1).reshape(own, fold * D)
    late = lax.all_gather(
        jnp.concatenate([inner_fold, outer_weight.reshape(own, fold * D), output_weight], axis=1),
        ("dp", "tile"), axis=0, tiled=True)
    early = early.reshape(2 * count, own + 8, 3 * D)
    qkv_full = early[:, :own].reshape(D, 3 * D)
    kinds = 8 + fold
    vec = early[:, own, :kinds * own].reshape(2 * count, kinds, own).transpose(1, 0, 2).reshape(kinds, D).astype(F32)
    vec = jnp.pad(vec, ((0, 16 - kinds), (0, 0)))

    keys, queries = mask_codes(segment_ids, valid, slots)
    code = jnp.where(valid, segment_ids, PAD_SLOTS)[None]
    offset = jnp.concatenate([vec[0], jnp.zeros((D,), F32), vec[1]])
    qkv = (dot(layer_input, qkv_full) + offset).astype(BF)
    lo, hi = key_ranges(segment_ids, valid, *FWD_TILES[:2])
    mixed, log_totals = attend_forward(qkv, lo, hi, keys, queries, HEADS, *FWD_TILES)
    numbers = jnp.pad(pair_slots.astype(BF), ((0, PAD_SLOTS - slots), (0, 126)), constant_values=-1)
    low, first, second, active, slope, layer_out, packets, counts = feed_forward(
        mixed, layer_input, code, numbers, vec, late, count, fold)
    packets = lax.all_to_all(packets, "dp", 0, 0, tiled=True).reshape(count * PAD_SLOTS, D + 128)
    loss_block, pooled_grad = contrast(packets, swap_tile(packets), counts, me, tile, slots)
    dim_losses = loss_block[0, :5]
    total_loss = jnp.sum(dim_losses)

    outer_grad, inner_grad, residual_grad, branch_grad, mixed_grad, sums = feed_backward(
        result_cotangent, code, pooled_grad, vec, first, second, slope, late, fold)
    feed = feed_weights(low, inner_grad, active, outer_grad, fold)
    feed_shard = lax.psum_scatter(feed, ("dp", "tile"), scatter_dimension=0, tiled=True).astype(F32)
    lo, hi = key_ranges(segment_ids, valid, *BWD_TILES[:2])
    query_grad, key_grad, value_grad = attend_backward(
        qkv, mixed_grad, mixed, log_totals.reshape(-1, 2 * BWD_TILES[2], rows), lo, hi, keys, queries, HEADS, *BWD_TILES)
    sums = jnp.concatenate(
        [jnp.sum(query_grad, axis=0, dtype=F32)[None], jnp.sum(value_grad, axis=0, dtype=F32)[None], sums[2:]], axis=0)
    vector_grads = jnp.pad(sums, ((0, 112), (0, 0))).T
    attention_grads = jnp.concatenate(
        [tn(layer_input, query_grad).astype(BF), tn(layer_input, key_grad).astype(BF),
         tn(layer_input, value_grad).astype(BF), tn(mixed, branch_grad).astype(BF), vector_grads.astype(BF)], axis=1)
    shard = scatter_rows(attention_grads)
    input_grad = (
        residual_grad + nt(query_grad, qkv_full[:, :D]) + nt(key_grad, qkv_full[:, D:2 * D])
        + nt(value_grad, qkv_full[:, 2 * D:]))
    small = shard[:, 4 * D:].T
    return (
        total_loss, dim_losses, layer_out, input_grad,
        shard[:, :D], shard[:, D:2 * D], shard[:, 2 * D:3 * D], shard[:, 3 * D:4 * D],
        small[0], small[1], small[2], small[3], small[4],
        feed_shard[:, :fold * D].reshape(own, fold, D).transpose(0, 2, 1).reshape(own, fold * D),
        small[8:8 + fold].T.reshape(own * fold),
        feed_shard[:, fold * D:].reshape(own * fold, D),
        small[5], small[6], small[7],
    )


def solution(mesh):
    both = ("dp", "tile")
    wide, flat = P(both, None), P(both)
    return jax.shard_map(
        shards,
        mesh=mesh,
        in_specs=(wide, flat, flat, P("dp", None), wide, wide, wide, wide, wide)
        + (flat,) * 5 + (wide, flat, wide) + (flat,) * 3,
        out_specs=(P(), P(), wide, wide, wide, wide, wide, wide) + (flat,) * 5 + (wide, flat, wide) + (flat,) * 3,
        check_vma=False,
    )
```
